768 devices in a mesh: row: 96 (over z, y), col: 8 (over x, core).
Axes of the slice: x: 4, y: 8, z: 12, core: 2. Of those that a mesh axis runs over, the one named last changes fastest.
Arguments:
- weight: bfloat16 [9216, 27648], P('row', 'col'), may hold values from -6 to 6
- gradient: bfloat16 [9216, 27648], P('row', 'col'), may hold values from -150 to 150
- momentum: float32 [9216, 27648], P('row', 'col'), may hold values from -6 to 6
- right_factor: bfloat16 [27648, 256], P(('col', 'row')), may hold values from -6 to 6
Outputs:
- new_weight: bfloat16 [9216, 27648], P('row', 'col')
- new_momentum: float32 [9216, 27648], P('row', 'col')
- new_right: bfloat16 [27648, 256], P(('col', 'row'))
The draws below stay inside these ranges and needn't reach their ends.
All inputs are finite; a program needn't handle non-finite values.
Results may differ from the reference program's by a relative error of at most 0.0063.
Values may be sent and summed in bfloat16 or wider, within the bound.
No kernel may reach another device: no remote copies, remote signals or barrier semaphores. Data moves between devices by JAX's collectives and lax.ppermute only.
A program may use at most 32 MiB of HBM per device.

```python
import math
import jax
import jax.numpy as jnp
from jax import lax

ROWS = 9216
COLS = 27648
RANK = 256


def draw_gradient(key, part):
    key_row, key_col, key_base = jax.random.split(key, 3)
    row_pos = jnp.arange(ROWS, dtype=jnp.float32) / ROWS
    col_pos = jnp.arange(COLS, dtype=jnp.float32) / COLS
    row_scale = jnp.exp((row_pos - 0.5) * math.log(3.0) + jax.random.uniform(key_row, (ROWS,), minval=-0.5, maxval=0.5) * math.log(10.0))
    col_scale = jnp.exp((col_pos - 0.5) * math.log(3.0) + jax.random.uniform(key_col, (COLS,), minval=-0.5, maxval=0.5) * math.log(10.0))
    base_part = jax.random.truncated_normal(key_base, -4.0, 4.0, (ROWS, COLS))
    return (base_part * row_scale[:, None] * col_scale[None, :]).astype(jnp.bfloat16)


def block_levels(stream_key, shape, cuts, smallest, largest):
    gain = 1.0
    for axis_at, parts in cuts:
        steps = jax.random.uniform(jax.random.fold_in(jax.random.fold_in(stream_key, 6), axis_at), (parts,), jnp.float32, smallest / len(cuts), largest / len(cuts))
        gain = gain * jnp.repeat(jnp.exp(steps), shape[axis_at] // parts).reshape((-1,) + (1,) * (len(shape) - 1 - axis_at))
    return gain


def centred(rng, extent, deviation, limit, shards=(), kind=jnp.bfloat16):
    factor_of = block_levels(rng, extent, shards, -0.22, 0.18) if shards else 1.0
    array = jax.random.normal(rng, extent, jnp.float32) * deviation * factor_of
    return jnp.minimum(jnp.maximum(array, -limit), limit).astype(kind)


def setup_inputs(seed: int = 0) -> dict:
    arg_keys = jax.random.split(jax.random.key(seed), 5)
    weight = centred(arg_keys[0], (ROWS, COLS), 1.0, 6.0, ((0, 96), (1, 8)))
    gradient = draw_gradient(jax.random.fold_in(arg_keys[4], 71), 0)
    momentum = centred(arg_keys[2], (ROWS, COLS), 1.0, 6.0, ((0, 96), (1, 8)), jnp.float32)
    right_factor = centred(arg_keys[3], (COLS, RANK), 1.0, 6.0, ((0, 768),))
    return dict(weight=weight, gradient=gradient, momentum=momentum, right_factor=right_factor)


shift_frac = 0.001
epsilon = 1e-06
feedback = 0.05
step_size = 0.5

def orthonormal(left_rows, gram):
    shift = shift_frac * jnp.trace(gram) / gram.shape[0]
    lower = jnp.linalg.cholesky(gram + shift * jnp.eye(gram.shape[0], dtype=gram.dtype))
    return lax.linalg.triangular_solve(lower, left_rows, left_side=False, lower=True, transpose_a=True)

def reference(weight, gradient, momentum, right_factor):
    buffer = momentum + gradient.astype(jnp.float32)
    buffer_low = buffer.astype(jnp.bfloat16)
    left = jnp.dot(buffer_low.astype(jnp.float32), right_factor.astype(jnp.float32), preferred_element_type=jnp.float32) / math.sqrt(COLS)
    gram = jnp.dot(left.T, left, precision=lax.Precision.HIGHEST)
    left_low = orthonormal(left, gram).astype(jnp.bfloat16)
    right = lax.dot_general(buffer_low.astype(jnp.float32), left_low.astype(jnp.float32), (((0,), (0,)), ((), ())), preferred_element_type=jnp.float32)
    colsq = lax.optimization_barrier(jnp.sum(right * right, axis=0))
    spread = jnp.sqrt(colsq / COLS + epsilon)
    new_right = (right / spread).astype(jnp.bfloat16)
    left_feed = (left_low.astype(jnp.float32) * spread).astype(jnp.bfloat16)
    feed_term = lax.dot_general(left_feed.astype(jnp.float32), new_right.astype(jnp.float32), (((1,), (1,)), ((), ())), preferred_element_type=jnp.float32)
    new_momentum = buffer - feedback * feed_term
    step_term = lax.dot_general(left_low.astype(jnp.float32), new_right.astype(jnp.float32), (((1,), (1,)), ((), ())), preferred_element_type=jnp.float32)
    new_weight = (weight.astype(jnp.float32) - step_size * math.sqrt(ROWS / RANK) * step_term).astype(jnp.bfloat16)
    return (new_weight, new_momentum, new_right)
```

```python
import math

import jax
import jax.numpy as jnp
from jax import lax
from jax.sharding import Mesh, PartitionSpec as P

ROWS = 9216
COLS = 27648
RANK = 256

shift_frac = 0.001
epsilon = 1e-06
feedback = 0.05
step_size = 0.5

NZ, NY, NX, NC = 12, 8, 4, 2
SLAB = ("y", "x", "c")
NSLAB = NY * NX * NC


def orthonormal(left_rows, gram):
    shift = shift_frac * jnp.trace(gram) / gram.shape[0]
    lower = jnp.linalg.cholesky(gram + shift * jnp.eye(gram.shape[0], dtype=gram.dtype))
    return lax.linalg.triangular_solve(
        lower, left_rows, left_side=False, lower=True, transpose_a=True
    )


def gather(x, axes, n):
    return lax.all_to_all(jnp.broadcast_to(x[None], (n,) + x.shape), axes, 0, 0)


def halves(x):
    return jnp.concatenate([x[:, :128], x[:, 128:]], axis=0)


def unhalves(x):
    n = x.shape[0] // 2
    return jnp.concatenate([x[:n], x[n:]], axis=1)


def to_work():
    pairs = []
    for z in range(NZ):
        for y in range(NY):
            k = y * NZ + z
            pairs.append((k, z * NY + y))
    return pairs


def local(weight, gradient, momentum, right_factor):
    y_at = lax.axis_index("y")
    slab_at = (y_at * NX + lax.axis_index("x")) * NC + lax.axis_index("c")
    buffer = momentum + gradient.astype(jnp.float32)
    buffer_low = buffer.astype(jnp.bfloat16)
    rows, cols = buffer.shape
    wide = cols // NY

    old = lax.ppermute(right_factor, ("z", "y"), to_work())
    old = gather(old, "z", NZ).reshape(wide, RANK)

    tall = lax.all_to_all(
        buffer_low.reshape(rows, NY, wide).transpose(1, 0, 2), "y", 0, 0
    ).reshape(NY * rows, wide)

    part = jnp.dot(tall, old, preferred_element_type=jnp.float32)
    piece = 2 * NY * rows // NSLAB
    part = lax.all_to_all(halves(part).reshape(NSLAB, piece, 128), SLAB, 0, 0)
    own = jnp.sum(part, axis=0) / math.sqrt(COLS)
    left = unhalves(gather(own, SLAB, NSLAB).reshape(NSLAB * piece, 128))

    gram = jnp.dot(left.T, left, precision=lax.Precision.HIGHEST)
    gpiece = 2 * RANK // NSLAB
    mine = lax.dynamic_index_in_dim(
        halves(gram).reshape(NSLAB, gpiece, 128), slab_at, 0, keepdims=False
    )
    mine = jnp.sum(gather(mine, "z", NZ), axis=0)
    gram = unhalves(gather(mine, SLAB, NSLAB).reshape(2 * RANK, 128))

    left_low = orthonormal(left, gram).astype(jnp.bfloat16)

    right = lax.dot_general(
        tall, left_low, (((0,), (0,)), ((), ())), preferred_element_type=jnp.float32
    )
    right = right.astype(jnp.bfloat16).reshape(NZ, wide // NZ, RANK)
    right = jnp.sum(lax.all_to_all(right, "z", 0, 0).astype(jnp.float32), axis=0)

    sent = gather(right.astype(jnp.bfloat16), "z", NZ).reshape(wide, RANK)
    sent = gather(sent, "y", NY).reshape(cols, RANK)
    wide_sent = sent.astype(jnp.float32)
    colsq = jnp.sum(wide_sent * wide_sent, axis=0)
    colsq = jnp.sum(
        gather(jnp.pad(colsq.reshape(2, 128), ((0, 6), (0, 0))), ("x", "c"), NX * NC), axis=0
    )
    colsq = colsq[:2].reshape(RANK)
    spread = jnp.sqrt(colsq / COLS + epsilon)
    new_right = (right / spread).astype(jnp.bfloat16)
    new_right = lax.ppermute(new_right, ("z", "y"), [(b, a) for a, b in to_work()])

    mine_low = lax.dynamic_slice_in_dim(left_low, y_at * rows, rows, 0)
    scaled = (mine_low.astype(jnp.float32) / spread).astype(jnp.bfloat16)
    step_scale = step_size * math.sqrt(ROWS / RANK)
    nt = (((1,), (1,)), ((), ()))
    feed_term = lax.dot_general(mine_low, sent, nt, preferred_element_type=jnp.float32)
    step_term = lax.dot_general(scaled, sent, nt, preferred_element_type=jnp.float32)
    new_momentum = buffer - feedback * feed_term
    new_weight = (weight.astype(jnp.float32) - step_scale * step_term).astype(jnp.bfloat16)
    return (new_weight, new_momentum, new_right)


def solution(mesh):
    grid = Mesh(mesh.devices.reshape(NZ, NY, NX, NC), ("z", "y", "x", "c"))
    row, col = ("z", "y"), ("x", "c")
    placed = (P(row, col), P(row, col), P(row, col), P(col + row, None))
    return jax.shard_map(
        local,
        mesh=grid,
        in_specs=placed,
        out_specs=(P(row, col), P(row, col), P(col + row, None)),
        check_vma=False,
    )
```

```python
import math

import jax
import jax.numpy as jnp
from jax import lax
from jax.experimental import pallas as pl
from jax.experimental.pallas import tpu as pltpu
from jax.sharding import Mesh, PartitionSpec as P

ROWS = 9216
COLS = 27648
RANK = 256

shift_frac = 0.001
epsilon = 1e-06
feedback = 0.05
step_size = 0.5

NZ, NY, NX, NC = 12, 8, 4, 2
SLAB = ("y", "x", "c")
NSLAB = NY * NX * NC


HALF = 128
GROUP = 4


def inverse_lower(block):
    tiles = HALF // 8
    at = lax.broadcasted_iota(jnp.int32, (8, HALF), 0)
    lane = lax.broadcasted_iota(jnp.int32, (8, HALF), 1)
    a = [block[8 * t : 8 * t + 8] for t in range(tiles)]
    w = [jnp.where(lane == at + 8 * t, 1.0, 0.0) for t in range(tiles)]
    roots = [jnp.zeros((8, HALF), jnp.float32) for t in range(tiles)]
    full = lambda v: jnp.broadcast_to(v, (8, HALF))
    for k in range(0, HALF, GROUP):
        own, base = k // 8, k % 8
        r = [full(a[own][base + j : base + j + 1]) for j in range(GROUP)]
        v = [full(w[own][base + j : base + j + 1]) for j in range(GROUP)]
        s = {}
        for i in range(GROUP):
            for j in range(i, GROUP):
                s[i, j] = full(r[i][:, k + j : k + j + 1])
        c = {}
        for t in range(own, tiles):
            for j in range(GROUP):
                c[t, j] = full(a[t][:, k + j : k + j + 1])
        inv = []
        for j in range(GROUP):
            inv.append(1.0 / s[j, j])
            for i in range(j + 1, GROUP):
                f = s[j, i] * inv[j]
                for m in range(i, GROUP):
                    s[i, m] = s[i, m] - f * s[j, m]
                r[i] = r[i] - f * r[j]
                v[i] = v[i] - f * v[j]
            roots[own] = jnp.where(at == base + j, lax.rsqrt(s[j, j]), roots[own])
        for t in range(own, tiles):
            l = []
            for j in range(GROUP):
                x = c[t, j]
                for i in range(j):
                    x = x - l[i] * s[i, j]
                x = x * inv[j]
                if t == own:
                    x = jnp.where(at > base + j, x, 0.0)
                l.append(x)
            for j in range(GROUP):
                a[t] = a[t] - l[j] * r[j]
                w[t] = w[t] - l[j] * v[j]
    return jnp.concatenate([w[t] * roots[t] for t in range(tiles)], axis=0)

def dot(x, y, dims):
    return lax.dot_general(x, y, (dims, ((), ())), precision=lax.Precision.HIGHEST, preferred_element_type=jnp.float32)

def kernel(g_ref, out_ref, work_ref, inv_ref):
    n = 2 * HALF
    row = lax.broadcasted_iota(jnp.int32, (HALF, HALF), 0)
    eye = row == lax.broadcasted_iota(jnp.int32, (HALF, HALF), 1)
    diag = jnp.where(eye, g_ref[0:HALF, :] + g_ref[3 * HALF :, :], 0.0)
    shift = shift_frac * jnp.sum(diag) / n
    work_ref[...] = g_ref[0:HALF, :] + jnp.where(eye, shift, 0.0)
    def step(b, carry):
        inv_ref[pl.ds(b * HALF, HALF), :] = inverse_lower(work_ref[...])
        @pl.when(b == 0)
        def _():
            z = dot(inv_ref[0:HALF, :], g_ref[2 * HALF : 3 * HALF, :], ((1,), (0,)))
            out_ref[HALF:, 0:HALF] = dot(z, inv_ref[0:HALF, :], ((0,), (0,)))
            work_ref[...] = g_ref[3 * HALF :, :] + jnp.where(eye, shift, 0.0) - dot(z, z, ((0,), (0,)))
        return carry
    lax.fori_loop(0, 2, step, 0)
    out_ref[0:HALF, 0:HALF] = inv_ref[0:HALF, :]
    out_ref[0:HALF, HALF:] = jnp.zeros((HALF, HALF), jnp.float32)
    out_ref[HALF:, HALF:] = inv_ref[HALF:, :]
    out_ref[HALF:, 0:HALF] = -dot(inv_ref[HALF:, :], out_ref[HALF:, 0:HALF], ((1,), (0,)))

def lower_inverse(g):
    return pl.pallas_call(kernel, out_shape=jax.ShapeDtypeStruct((256,256), jnp.float32),
        scratch_shapes=[pltpu.VMEM((HALF,HALF),jnp.float32), pltpu.VMEM((2*HALF,HALF),jnp.float32)],
        name="lower_inverse")(g)


def gather(x, axes, n):
    return lax.all_to_all(jnp.broadcast_to(x[None], (n,) + x.shape), axes, 0, 0)


def halves(x):
    return jnp.concatenate([x[:, :128], x[:, 128:]], axis=0)


def unhalves(x):
    n = x.shape[0] // 2
    return jnp.concatenate([x[:n], x[n:]], axis=1)


def to_work():
    pairs = []
    for z in range(NZ):
        for y in range(NY):
            k = y * NZ + z
            pairs.append((k, z * NY + y))
    return pairs


def local(weight, gradient, momentum, right_factor):
    y_at = lax.axis_index("y")
    slab_at = (y_at * NX + lax.axis_index("x")) * NC + lax.axis_index("c")
    buffer = momentum + gradient.astype(jnp.float32)
    buffer_low = buffer.astype(jnp.bfloat16)
    rows, cols = buffer.shape
    wide = cols // NY

    old = lax.ppermute(right_factor, ("z", "y"), to_work())
    old = gather(old, "z", NZ).reshape(wide, RANK)

    tall = lax.all_to_all(
        buffer_low.reshape(rows, NY, wide).transpose(1, 0, 2), "y", 0, 0
    ).reshape(NY * rows, wide)

    part = jnp.dot(tall, old, preferred_element_type=jnp.float32)
    piece = 2 * NY * rows // NSLAB
    part = lax.all_to_all(halves(part).reshape(NSLAB, piece, 128), SLAB, 0, 0)
    own = jnp.sum(part, axis=0) / math.sqrt(COLS)
    left = unhalves(gather(own, SLAB, NSLAB).reshape(NSLAB * piece, 128))

    gram = jnp.dot(left.T, left, precision=lax.Precision.HIGHEST)
    gpiece = 2 * RANK // NSLAB
    mine = lax.dynamic_index_in_dim(
        halves(gram).reshape(NSLAB, gpiece, 128), slab_at, 0, keepdims=False
    )
    mine = jnp.sum(gather(mine, "z", NZ), axis=0)
    gram = gather(mine, SLAB, NSLAB).reshape(2 * RANK, 128)

    left_low = dot(left, lower_inverse(gram), ((1,), (1,))).astype(jnp.bfloat16)

    right = lax.dot_general(
        tall, left_low, (((0,), (0,)), ((), ())), preferred_element_type=jnp.float32
    )
    right = right.astype(jnp.bfloat16).reshape(NZ, wide // NZ, RANK)
    right = jnp.sum(lax.all_to_all(right, "z", 0, 0).astype(jnp.float32), axis=0)

    sent = gather(right.astype(jnp.bfloat16), "z", NZ).reshape(wide, RANK)
    sent = gather(sent, "y", NY).reshape(cols, RANK)
    wide_sent = sent.astype(jnp.float32)
    colsq = jnp.sum(wide_sent * wide_sent, axis=0)
    colsq = jnp.sum(
        gather(jnp.pad(colsq.reshape(2, 128), ((0, 6), (0, 0))), ("x", "c"), NX * NC), axis=0
    )
    colsq = colsq[:2].reshape(RANK)
    spread = jnp.sqrt(colsq / COLS + epsilon)
    new_right = (right / spread).astype(jnp.bfloat16)
    new_right = lax.ppermute(new_right, ("z", "y"), [(b, a) for a, b in to_work()])

    mine_low = lax.dynamic_slice_in_dim(left_low, y_at * rows, rows, 0)
    scaled = (mine_low.astype(jnp.float32) / spread).astype(jnp.bfloat16)
    step_scale = step_size * math.sqrt(ROWS / RANK)
    nt = (((1,), (1,)), ((), ()))
    feed_term = lax.dot_general(mine_low, sent, nt, preferred_element_type=jnp.float32)
    step_term = lax.dot_general(scaled, sent, nt, preferred_element_type=jnp.float32)
    new_momentum = buffer - feedback * feed_term
    new_weight = (weight.astype(jnp.float32) - step_scale * step_term).astype(jnp.bfloat16)
    return (new_weight, new_momentum, new_right)


def solution(mesh):
    grid = Mesh(mesh.devices.reshape(NZ, NY, NX, NC), ("z", "y", "x", "c"))
    row, col = ("z", "y"), ("x", "c")
    placed = (P(row, col), P(row, col), P(row, col), P(col + row, None))
    return jax.shard_map(
        local,
        mesh=grid,
        in_specs=placed,
        out_specs=(P(row, col), P(row, col), P(col + row, None)),
        check_vma=False,
    )
```

```python
import math

import jax
import jax.numpy as jnp
from jax import lax
from jax.experimental import pallas as pl
from jax.experimental.pallas import tpu as pltpu
from jax.sharding import Mesh, PartitionSpec as P

ROWS = 9216
COLS = 27648
RANK = 256

shift_frac = 0.001
epsilon = 1e-06
feedback = 0.05
step_size = 0.5

NZ, NY, NX, NC = 12, 8, 4, 2
SLAB = ("y", "x", "c")
NSLAB = NY * NX * NC


HALF = 128
GROUP = 4


def inverse_lower(block):
    tiles = HALF // 8
    at = lax.broadcasted_iota(jnp.int32, (8, HALF), 0)
    lane = lax.broadcasted_iota(jnp.int32, (8, HALF), 1)
    a = [block[8 * t : 8 * t + 8] for t in range(tiles)]
    w = [jnp.where(lane == at + 8 * t, 1.0, 0.0) for t in range(tiles)]
    roots = [jnp.zeros((8, HALF), jnp.float32) for t in range(tiles)]
    full = lambda v: jnp.broadcast_to(v, (8, HALF))
    for k in range(0, HALF, GROUP):
        own, base = k // 8, k % 8
        r = [full(a[own][base + j : base + j + 1]) for j in range(GROUP)]
        v = [full(w[own][base + j : base + j + 1]) for j in range(GROUP)]
        s = {}
        for i in range(GROUP):
            for j in range(i, GROUP):
                s[i, j] = full(r[i][:, k + j : k + j + 1])
        c = {}
        for t in range(own, tiles):
            for j in range(GROUP):
                c[t, j] = full(a[t][:, k + j : k + j + 1])
        inv = []
        for j in range(GROUP):
            inv.append(1.0 / s[j, j])
            for i in range(j + 1, GROUP):
                f = s[j, i] * inv[j]
                for m in range(i, GROUP):
                    s[i, m] = s[i, m] - f * s[j, m]
                r[i] = r[i] - f * r[j]
                v[i] = v[i] - f * v[j]
            roots[own] = jnp.where(at == base + j, lax.rsqrt(s[j, j]), roots[own])
        for t in range(own, tiles):
            l = []
            for j in range(GROUP):
                x = c[t, j]
                for i in range(j):
                    x = x - l[i] * s[i, j]
                x = x * inv[j]
                if t == own:
                    x = jnp.where(at > base + j, x, 0.0)
                l.append(x)
            for j in range(GROUP):
                a[t] = a[t] - l[j] * r[j]
                w[t] = w[t] - l[j] * v[j]
    return jnp.concatenate([w[t] * roots[t] for t in range(tiles)], axis=0)

def dot(x, y, dims):
    return lax.dot_general(x, y, (dims, ((), ())), precision=lax.Precision.HIGHEST, preferred_element_type=jnp.float32)

def kernel(g_ref, out_ref, work_ref, inv_ref):
    n = 2 * HALF
    row = lax.broadcasted_iota(jnp.int32, (HALF, HALF), 0)
    eye = row == lax.broadcasted_iota(jnp.int32, (HALF, HALF), 1)
    diag = jnp.where(eye, g_ref[0:HALF, :] + g_ref[3 * HALF :, :], 0.0)
    shift = shift_frac * jnp.sum(diag) / n
    work_ref[...] = g_ref[0:HALF, :] + jnp.where(eye, shift, 0.0)
    def step(b, carry):
        inv_ref[pl.ds(b * HALF, HALF), :] = inverse_lower(work_ref[...])
        @pl.when(b == 0)
        def _():
            z = dot(inv_ref[0:HALF, :], g_ref[2 * HALF : 3 * HALF, :], ((1,), (0,)))
            out_ref[HALF:, 0:HALF] = dot(z, inv_ref[0:HALF, :], ((0,), (0,)))
            work_ref[...] = g_ref[3 * HALF :, :] + jnp.where(eye, shift, 0.0) - dot(z, z, ((0,), (0,)))
        return carry
    lax.fori_loop(0, 2, step, 0)
    out_ref[0:HALF, 0:HALF] = inv_ref[0:HALF, :]
    out_ref[0:HALF, HALF:] = jnp.zeros((HALF, HALF), jnp.float32)
    out_ref[HALF:, HALF:] = inv_ref[HALF:, :]
    out_ref[HALF:, 0:HALF] = -dot(inv_ref[HALF:, :], out_ref[HALF:, 0:HALF], ((1,), (0,)))

def lower_inverse(g):
    return pl.pallas_call(kernel, out_shape=jax.ShapeDtypeStruct((256,256), jnp.float32),
        scratch_shapes=[pltpu.VMEM((HALF,HALF),jnp.float32), pltpu.VMEM((2*HALF,HALF),jnp.float32)],
        name="lower_inverse")(g)


def gather(x, axes, n):
    return lax.all_to_all(jnp.broadcast_to(x[None], (n,) + x.shape), axes, 0, 0)


def halves(x):
    return jnp.concatenate([x[:, :128], x[:, 128:]], axis=0)


def unhalves(x):
    n = x.shape[0] // 2
    return jnp.concatenate([x[:n], x[n:]], axis=1)


def to_work():
    pairs = []
    for z in range(NZ):
        for y in range(NY):
            k = y * NZ + z
            pairs.append((k, z * NY + y))
    return pairs


def shift(x, by):
    return lax.ppermute(x, "y", [(i, (i + by) % NY) for i in range(NY)])


FROM = ((-3, 0, 3), (-4, -1, 2), (-2, 1))


def spread_y(x):
    first = jnp.stack([shift(x, 3), x, shift(x, -3)])
    return first, shift(first, 1), shift(first[:2], -1)


def update(y_ref, first, second, third, low, spread, weight, gradient, momentum, new_weight, new_momentum, right, both):
    wide = first.shape[1]
    rows = low.shape[0]

    @pl.when(pl.program_id(0) == 0)
    def _():
        for blocks, places in zip((first, second, third), FROM):
            for j, place in enumerate(places):
                block = lax.rem(y_ref[0] + (place + NY), NY)
                right[pl.ds(pl.multiple_of(block * wide, 16), wide), :] = blocks[j]
        both[0:rows, :] = low[...]
        both[rows:, :] = (low[...].astype(jnp.float32) / spread[...]).astype(jnp.bfloat16)

    cols = weight.shape[1]
    at = pl.multiple_of(pl.program_id(0) * cols, 128)
    terms = lax.dot_general(
        both[...], right[pl.ds(at, cols), :], (((1,), (1,)), ((), ())), preferred_element_type=jnp.float32
    )
    buffer = momentum[...] + gradient[...].astype(jnp.float32)
    new_momentum[...] = buffer - feedback * terms[:rows]
    step_scale = step_size * math.sqrt(ROWS / RANK)
    new_weight[...] = (weight[...].astype(jnp.float32) - step_scale * terms[rows:]).astype(jnp.bfloat16)


def updated(y_at, blocks, low, spread, weight, gradient, momentum, steps=3):
    rows, cols = weight.shape
    whole = lambda x: pl.BlockSpec(x.shape, lambda i: (0,) * x.ndim)
    part = pl.BlockSpec((rows, cols // steps), lambda i: (0, i))
    return pl.pallas_call(
        update,
        grid=(steps,),
        in_specs=[pl.BlockSpec(memory_space=pltpu.SMEM)]
        + [whole(x) for x in (*blocks, low, spread)]
        + [part, part, part],
        out_specs=[part, part],
        out_shape=[
            jax.ShapeDtypeStruct((rows, cols), jnp.bfloat16),
            jax.ShapeDtypeStruct((rows, cols), jnp.float32),
        ],
        scratch_shapes=[
            pltpu.VMEM((cols, RANK), jnp.bfloat16),
            pltpu.VMEM((2 * rows, RANK), jnp.bfloat16),
        ],
        name="update",
    )(y_at.astype(jnp.int32).reshape(1), *blocks, low, spread, weight, gradient, momentum)


def local(weight, gradient, momentum, right_factor):
    y_at = lax.axis_index("y")
    slab_at = (y_at * NX + lax.axis_index("x")) * NC + lax.axis_index("c")
    buffer_low = (momentum + gradient.astype(jnp.float32)).astype(jnp.bfloat16)
    rows, cols = buffer_low.shape
    wide = cols // NY

    old = lax.ppermute(right_factor, ("z", "y"), to_work())
    old = gather(old, "z", NZ).reshape(wide, RANK)

    tall = lax.all_to_all(
        buffer_low.reshape(rows, NY, wide).transpose(1, 0, 2), "y", 0, 0
    ).reshape(NY * rows, wide)

    part = jnp.dot(tall, old, preferred_element_type=jnp.float32)
    part = jnp.sum(lax.all_to_all(part.reshape(NC, -1, RANK), "c", 0, 0), axis=0)
    chips = NY * NX
    part = lax.all_to_all(halves(part).reshape(chips, -1, 128), ("y", "x"), 0, 0)
    own = jnp.sum(part, axis=0) / math.sqrt(COLS)
    left = unhalves(gather(own, ("y", "x"), chips).reshape(-1, 128))
    left = gather(left, "c", NC).reshape(-1, RANK)

    gram = jnp.dot(left.T, left, precision=lax.Precision.HIGHEST)
    gpiece = 2 * RANK // NSLAB
    mine = lax.dynamic_index_in_dim(
        halves(gram).reshape(NSLAB, gpiece, 128), slab_at, 0, keepdims=False
    )
    mine = jnp.sum(gather(mine, "z", NZ), axis=0)
    gram = gather(mine, SLAB, NSLAB).reshape(2 * RANK, 128)

    left_low = dot(left, lower_inverse(gram), ((1,), (1,))).astype(jnp.bfloat16)

    right = lax.dot_general(
        tall, left_low, (((0,), (0,)), ((), ())), preferred_element_type=jnp.float32
    )
    right = right.astype(jnp.bfloat16).reshape(NZ, wide // NZ, RANK)
    right = jnp.sum(lax.all_to_all(right, "z", 0, 0).astype(jnp.float32), axis=0)

    sent = gather(right.astype(jnp.bfloat16), "z", NZ).reshape(wide, RANK)
    blocks = spread_y(sent)
    squares = sent.astype(jnp.float32)
    squares = jnp.sum(squares * squares, axis=0).reshape(2, 128)
    colsq = jnp.sum(gather(jnp.pad(squares, ((0, 6), (0, 0))), SLAB, NSLAB), axis=0)
    spread = jnp.sqrt(colsq[:2].reshape(1, RANK) / COLS + epsilon)

    new_right = (right / spread).astype(jnp.bfloat16)
    new_right = lax.ppermute(new_right, ("z", "y"), [(b, a) for a, b in to_work()])
    mine_low = lax.dynamic_slice_in_dim(left_low, y_at * rows, rows, 0)
    new_weight, new_momentum = updated(y_at, blocks, mine_low, spread, weight, gradient, momentum)
    return (new_weight, new_momentum, new_right)


def solution(mesh):
    grid = Mesh(mesh.devices.reshape(NZ, NY, NX, NC), ("z", "y", "x", "c"))
    row, col = ("z", "y"), ("x", "c")
    placed = (P(row, col), P(row, col), P(row, col), P(col + row, None))
    return jax.shard_map(
        local,
        mesh=grid,
        in_specs=placed,
        out_specs=(P(row, col), P(row, col), P(col + row, None)),
        check_vma=False,
    )
```

```python
import math

import jax
import jax.numpy as jnp
from jax import lax
from jax.experimental import pallas as pl
from jax.experimental.pallas import tpu as pltpu
from jax.sharding import Mesh, PartitionSpec as P


ROWS = 9216
COLS = 27648
RANK = 256

shift_frac = 0.001
epsilon = 1e-06
feedback = 0.05
step_size = 0.5

NZ, NY, NX, NC = 12, 8, 4, 2
SLAB = ("y", "x", "c")
NSLAB = NY * NX * NC


HALF = 128
GROUP = 8


def inverse_lower(block):
    tiles = HALF // 8
    at = lax.broadcasted_iota(jnp.int32, (8, HALF), 0)
    lane = lax.broadcasted_iota(jnp.int32, (8, HALF), 1)
    a = [block[8 * t : 8 * t + 8] for t in range(tiles)]
    w = [jnp.where(lane == at + 8 * t, 1.0, 0.0) for t in range(tiles)]
    roots = [jnp.zeros((8, HALF), jnp.float32) for _ in range(tiles)]
    full = lambda v: jnp.broadcast_to(v, (8, HALF))
    for k in range(0, HALF, GROUP):
        own, base = k // 8, k % 8
        r = [full(a[own][base + j : base + j + 1]) for j in range(GROUP)]
        v = [full(w[own][base + j : base + j + 1]) for j in range(GROUP)]
        s = {}
        for i in range(GROUP):
            for j in range(i, GROUP):
                s[i, j] = full(r[i][:, k + j : k + j + 1])
        c = {}
        for t in range(own, tiles):
            for j in range(GROUP):
                c[t, j] = full(a[t][:, k + j : k + j + 1])
        inv = []
        for j in range(GROUP):
            if j % 2:
                inv.append(after)
            else:
                inv.append(1.0 / s[j, j])
                after = s[j, j] / (s[j, j] * s[j + 1, j + 1] - s[j, j + 1] * s[j, j + 1])
            for i in range(j + 1, GROUP):
                f = s[j, i] * inv[j]
                for m in range(i, GROUP):
                    s[i, m] = s[i, m] - f * s[j, m]
                r[i] = r[i] - f * r[j]
                v[i] = v[i] - f * v[j]
            roots[own] = jnp.where(at == base + j, jnp.sqrt(inv[j]), roots[own])
        for t in range(own, tiles):
            l = []
            for j in range(GROUP):
                x = c[t, j]
                for i in range(j):
                    x = x - l[i] * s[i, j]
                x = x * inv[j]
                if t == own:
                    x = jnp.where(at > base + j, x, 0.0)
                l.append(x)
            for j in range(GROUP):
                a[t] = a[t] - l[j] * r[j]
                w[t] = w[t] - l[j] * v[j]
    return jnp.concatenate([w[t] * roots[t] for t in range(tiles)], axis=0)


def dot(x, y, dims):
    return lax.dot_general(x, y, (dims, ((), ())), precision=lax.Precision.HIGHEST, preferred_element_type=jnp.float32)


def kernel(g_ref, out_ref, work_ref, inv_ref):
    first, across, last = (g_ref.at[k * HALF : (k + 1) * HALF] for k in range(3))
    row = lax.broadcasted_iota(jnp.int32, (HALF, HALF), 0)
    eye = row == lax.broadcasted_iota(jnp.int32, (HALF, HALF), 1)
    alpha = (2 * HALF) / jnp.sum(jnp.where(eye, first[...] + last[...], 0.0), keepdims=True)
    shifted = jnp.where(eye, shift_frac, 0.0)
    work_ref[...] = first[...] * alpha + shifted

    def step(b, carry):
        inv_ref[pl.ds(b * HALF, HALF), :] = inverse_lower(work_ref[...])

        @pl.when(b == 0)
        def _():
            z = dot(inv_ref[0:HALF, :], across[...] * alpha, ((1,), (0,)))
            out_ref[HALF:, 0:HALF] = dot(z, inv_ref[0:HALF, :], ((0,), (0,)))
            work_ref[...] = last[...] * alpha + shifted - dot(z, z, ((0,), (0,)))

        return carry

    lax.fori_loop(0, 2, step, 0)
    scale = jnp.sqrt(alpha)
    out_ref[0:HALF, 0:HALF] = inv_ref[0:HALF, :] * scale
    out_ref[0:HALF, HALF:] = jnp.zeros((HALF, HALF), jnp.float32)
    out_ref[HALF:, HALF:] = inv_ref[HALF:, :] * scale
    out_ref[HALF:, 0:HALF] = -scale * dot(inv_ref[HALF:, :], out_ref[HALF:, 0:HALF], ((1,), (0,)))


def lower_inverse(g):
    return pl.pallas_call(
        kernel,
        out_shape=jax.ShapeDtypeStruct((2 * HALF, 2 * HALF), jnp.float32),
        scratch_shapes=[
            pltpu.VMEM((HALF, HALF), jnp.float32),
            pltpu.VMEM((2 * HALF, HALF), jnp.float32),
        ],
        name="lower_inverse",
    )(g)


def gather(x, axes, n):
    return lax.all_to_all(jnp.broadcast_to(x[None], (n,) + x.shape), axes, 0, 0)


def halves(x):
    return jnp.concatenate([x[:, :128], x[:, 128:]], axis=0)


def unhalves(x):
    n = x.shape[0] // 2
    return jnp.concatenate([x[:n], x[n:]], axis=1)


def to_work():
    pairs = []
    for z in range(NZ):
        for y in range(NY):
            k = y * NZ + z
            pairs.append((k, z * NY + y))
    return pairs


def shift(x, by):
    return lax.ppermute(x, "y", [(i, (i + by) % NY) for i in range(NY)])


FROM = ((-3, 0, 3), (-4, -1, 2), (-2, 1))


def spread_y(x):
    above, below = shift(x, 3), shift(x, -3)
    first = jnp.stack([above, x, below])
    return first, shift(first, 1), shift(first[:2], -1)


def update(y_ref, first, second, third, low, spread, weight, gradient, momentum, new_weight, new_momentum, right, both):
    wide = first.shape[1]
    rows = low.shape[0]

    @pl.when(pl.program_id(0) == 0)
    def _():
        for blocks, places in zip((first, second, third), FROM):
            for j, place in enumerate(places):
                block = lax.rem(y_ref[0] + (place + NY), NY)
                right[pl.ds(pl.multiple_of(block * wide, 16), wide), :] = blocks[j]
        both[0:rows, :] = low[...]
        both[rows:, :] = (low[...].astype(jnp.float32) / spread[...]).astype(jnp.bfloat16)

    cols = weight.shape[1]
    at = pl.multiple_of(pl.program_id(0) * cols, 128)
    terms = lax.dot_general(
        both[...], right[pl.ds(at, cols), :], (((1,), (1,)), ((), ())), preferred_element_type=jnp.float32
    )
    buffer = momentum[...] + gradient[...].astype(jnp.float32)
    new_momentum[...] = buffer - feedback * terms[:rows]
    step_scale = step_size * math.sqrt(ROWS / RANK)
    new_weight[...] = (weight[...].astype(jnp.float32) - step_scale * terms[rows:]).astype(jnp.bfloat16)


def updated(y_at, blocks, low, spread, weight, gradient, momentum, steps=3):
    rows, cols = weight.shape
    whole = lambda x: pl.BlockSpec(x.shape, lambda i: (0,) * x.ndim)
    part = pl.BlockSpec((rows, cols // steps), lambda i: (0, i))
    return pl.pallas_call(
        update,
        grid=(steps,),
        in_specs=[pl.BlockSpec(memory_space=pltpu.SMEM)]
        + [whole(x) for x in (*blocks, low, spread)]
        + [part, part, part],
        out_specs=[part, part],
        out_shape=[
            jax.ShapeDtypeStruct((rows, cols), jnp.bfloat16),
            jax.ShapeDtypeStruct((rows, cols), jnp.float32),
        ],
        scratch_shapes=[
            pltpu.VMEM((cols, RANK), jnp.bfloat16),
            pltpu.VMEM((2 * rows, RANK), jnp.bfloat16),
        ],
        name="update",
    )(y_at.astype(jnp.int32).reshape(1), *blocks, low, spread, weight, gradient, momentum)


def step(weight, gradient, momentum, right_factor):
    y_at = lax.axis_index("y")
    buffer_low = (momentum + gradient.astype(jnp.float32)).astype(jnp.bfloat16)
    rows, cols = buffer_low.shape
    wide = cols // NY

    old = lax.ppermute(right_factor, ("z", "y"), to_work())
    old = gather(old, "z", NZ).reshape(wide, RANK)

    tall = lax.all_to_all(
        buffer_low.reshape(rows, NY, wide).transpose(1, 0, 2), "y", 0, 0
    ).reshape(NY * rows, wide)

    part = jnp.dot(tall, old, preferred_element_type=jnp.float32)
    part = jnp.sum(lax.all_to_all(part.reshape(NC, -1, RANK), "c", 0, 0), axis=0)
    chips = NY * NX
    part = lax.all_to_all(halves(part).reshape(chips, -1, 128), ("y", "x"), 0, 0)
    own = jnp.sum(part, axis=0) / math.sqrt(COLS)
    left = unhalves(gather(own, ("y", "x"), chips).reshape(-1, 128))
    left = gather(left, "c", NC).reshape(-1, RANK)

    gram = jnp.dot(left.T, left, precision=lax.Precision.HIGHEST)
    blocks = jnp.concatenate([gram[:HALF, :HALF], gram[:HALF, HALF:], gram[HALF:, HALF:]], axis=0)
    pieces = NY * NC
    mine = lax.dynamic_index_in_dim(
        blocks.reshape(pieces, -1, HALF), y_at * NC + lax.axis_index("c"), 0, keepdims=False
    )
    mine = jnp.sum(gather(mine, "z", NZ), axis=0)
    blocks = gather(mine, ("y", "c"), pieces).reshape(3 * HALF, HALF)

    left_low = dot(left, lower_inverse(blocks), ((1,), (1,))).astype(jnp.bfloat16)

    right = lax.dot_general(
        tall, left_low, (((0,), (0,)), ((), ())), preferred_element_type=jnp.float32
    )
    right = right.astype(jnp.bfloat16).reshape(NZ, wide // NZ, RANK)
    right = jnp.sum(lax.all_to_all(right, "z", 0, 0).astype(jnp.float32), axis=0)

    sent = gather(right.astype(jnp.bfloat16), "z", NZ).reshape(wide, RANK)
    blocks = spread_y(sent)
    squares = sent.astype(jnp.float32)
    squares = jnp.sum(squares * squares, axis=0).reshape(2, 128)
    colsq = jnp.sum(gather(jnp.pad(squares, ((0, 6), (0, 0))), SLAB, NSLAB), axis=0)
    spread = jnp.sqrt(colsq[:2].reshape(1, RANK) / COLS + epsilon)

    new_right = (right / spread).astype(jnp.bfloat16)
    new_right = lax.ppermute(new_right, ("z", "y"), [(b, a) for a, b in to_work()])
    mine_low = lax.dynamic_slice_in_dim(left_low, y_at * rows, rows, 0)
    new_weight, new_momentum = updated(y_at, blocks, mine_low, spread, weight, gradient, momentum)
    return (new_weight, new_momentum, new_right)


def solution(mesh):
    grid = Mesh(mesh.devices.reshape(NZ, NY, NX, NC), ("z", "y", "x", "c"))
    row, col = ("z", "y"), ("x", "c")
    placed = (P(row, col), P(row, col), P(row, col), P(col + row, None))
    return jax.shard_map(
        step,
        mesh=grid,
        in_specs=placed,
        out_specs=(P(row, col), P(row, col), P(col + row, None)),
        check_vma=False,
    )
```

```python
import math

import jax
import jax.numpy as jnp
from jax import lax
from jax.experimental import pallas as pl
from jax.experimental.pallas import tpu as pltpu
from jax.sharding import Mesh, PartitionSpec as P


ROWS = 9216
COLS = 27648
RANK = 256

shift_frac = 0.001
epsilon = 1e-06
feedback = 0.05
step_size = 0.5

NZ, NY, NX, NC = 12, 8, 4, 2
SLAB = ("y", "x", "c")
NSLAB = NY * NX * NC


HALF = 128
GROUP = 8


def inverse_lower(block):
    tiles = HALF // 8
    at = lax.broadcasted_iota(jnp.int32, (8, HALF), 0)
    lane = lax.broadcasted_iota(jnp.int32, (8, HALF), 1)
    a = [block[8 * t : 8 * t + 8] for t in range(tiles)]
    w = [jnp.where(lane == at + 8 * t, 1.0, 0.0) for t in range(tiles)]
    roots = [jnp.zeros((8, HALF), jnp.float32) for _ in range(tiles)]
    full = lambda v: jnp.broadcast_to(v, (8, HALF))
    for k in range(0, HALF, GROUP):
        own, base = k // 8, k % 8
        r = [full(a[own][base + j : base + j + 1]) for j in range(GROUP)]
        v = [full(w[own][base + j : base + j + 1]) for j in range(GROUP)]
        s = {}
        for i in range(GROUP):
            for j in range(i, GROUP):
                s[i, j] = full(r[i][:, k + j : k + j + 1])
        c = {}
        for t in range(own, tiles):
            for j in range(GROUP):
                c[t, j] = full(a[t][:, k + j : k + j + 1])
        inv = []
        for j in range(GROUP):
            if j % 2:
                inv.append(after)
            else:
                inv.append(1.0 / s[j, j])
                after = s[j, j] / (s[j, j] * s[j + 1, j + 1] - s[j, j + 1] * s[j, j + 1])
            for i in range(j + 1, GROUP):
                f = s[j, i] * inv[j]
                for m in range(i, GROUP):
                    s[i, m] = s[i, m] - f * s[j, m]
                r[i] = r[i] - f * r[j]
                v[i] = v[i] - f * v[j]
            roots[own] = jnp.where(at == base + j, jnp.sqrt(inv[j]), roots[own])
        for t in range(own, tiles):
            l = []
            for j in range(GROUP):
                x = c[t, j]
                for i in range(j):
                    x = x - l[i] * s[i, j]
                x = x * inv[j]
                if t == own:
                    x = jnp.where(at > base + j, x, 0.0)
                l.append(x)
            for j in range(GROUP):
                a[t] = a[t] - l[j] * r[j]
                w[t] = w[t] - l[j] * v[j]
    return jnp.concatenate([w[t] * roots[t] for t in range(tiles)], axis=0)


def dot(x, y, dims):
    return lax.dot_general(x, y, (dims, ((), ())), precision=lax.Precision.HIGHEST, preferred_element_type=jnp.float32)


def kernel(g_ref, out_ref, work_ref, inv_ref):
    first, across, last = (g_ref.at[k * HALF : (k + 1) * HALF] for k in range(3))
    row = lax.broadcasted_iota(jnp.int32, (HALF, HALF), 0)
    eye = row == lax.broadcasted_iota(jnp.int32, (HALF, HALF), 1)
    alpha = (2 * HALF) / jnp.sum(jnp.where(eye, first[...] + last[...], 0.0), keepdims=True)
    shifted = jnp.where(eye, shift_frac, 0.0)
    work_ref[...] = first[...] * alpha + shifted

    def step(b, carry):
        inv_ref[pl.ds(b * HALF, HALF), :] = inverse_lower(work_ref[...])

        @pl.when(b == 0)
        def _():
            z = dot(inv_ref[0:HALF, :], across[...] * alpha, ((1,), (0,)))
            out_ref[HALF:, 0:HALF] = dot(z, inv_ref[0:HALF, :], ((0,), (0,)))
            work_ref[...] = last[...] * alpha + shifted - dot(z, z, ((0,), (0,)))

        return carry

    lax.fori_loop(0, 2, step, 0)
    scale = jnp.sqrt(alpha)
    out_ref[0:HALF, 0:HALF] = inv_ref[0:HALF, :] * scale
    out_ref[0:HALF, HALF:] = jnp.zeros((HALF, HALF), jnp.float32)
    out_ref[HALF:, HALF:] = inv_ref[HALF:, :] * scale
    out_ref[HALF:, 0:HALF] = -scale * dot(inv_ref[HALF:, :], out_ref[HALF:, 0:HALF], ((1,), (0,)))


def lower_inverse(g):
    return pl.pallas_call(
        kernel,
        out_shape=jax.ShapeDtypeStruct((2 * HALF, 2 * HALF), jnp.float32),
        scratch_shapes=[
            pltpu.VMEM((HALF, HALF), jnp.float32),
            pltpu.VMEM((2 * HALF, HALF), jnp.float32),
        ],
        name="lower_inverse",
    )(g)


def gather(x, axes, n):
    return lax.all_to_all(jnp.broadcast_to(x[None], (n,) + x.shape), axes, 0, 0)


def halves(x):
    return jnp.concatenate([x[:, :128], x[:, 128:]], axis=0)


def unhalves(x):
    n = x.shape[0] // 2
    return jnp.concatenate([x[:n], x[n:]], axis=1)


def to_work():
    pairs = []
    for z in range(NZ):
        for y in range(NY):
            k = y * NZ + z
            pairs.append((k, z * NY + y))
    return pairs


def shift(x, by):
    return lax.ppermute(x, "y", [(i, (i + by) % NY) for i in range(NY)])


CUT = 224


def spread_y(x):
    above, below = shift(x, 3), shift(x, -3)
    first = jnp.concatenate([above[CUT:], above[:CUT], x, below[CUT:], below[:CUT]], axis=0)
    rest = x.shape[0] - CUT
    return first, shift(first[rest:], 1), shift(first[:-CUT], -1)


def pieces_of(wide):
    rest = wide - CUT
    both = lambda at, place: [(at, rest, place, CUT), (at + rest, CUT, place, 0)]
    return (
        both(0, -3) + [(wide, wide, 0, 0)] + both(2 * wide, 3),
        [(0, CUT, -4, 0), (CUT, wide, -1, 0)] + both(CUT + wide, 2),
        both(0, -2) + [(wide, wide, 1, 0), (2 * wide, rest, 4, CUT)],
    )


def update(y_ref, first, second, third, low, spread, weight, gradient, momentum, new_weight, new_momentum, right, both):
    wide = first.shape[0] // 3
    rows = low.shape[0]

    @pl.when(pl.program_id(0) == 0)
    def _():
        for blocks, pieces in zip((first, second, third), pieces_of(wide)):
            for at, n, place, to in pieces:
                block = lax.rem(y_ref[0] + (place + NY), NY)
                right[pl.ds(pl.multiple_of(block * wide + to, 16), n), :] = blocks[at : at + n, :]
        both[0:rows, :] = low[...]
        both[rows:, :] = (low[...].astype(jnp.float32) / spread[...]).astype(jnp.bfloat16)

    cols = weight.shape[1]
    at = pl.multiple_of(pl.program_id(0) * cols, 128)
    terms = lax.dot_general(
        both[...], right[pl.ds(at, cols), :], (((1,), (1,)), ((), ())), preferred_element_type=jnp.float32
    )
    buffer = momentum[...] + gradient[...].astype(jnp.float32)
    new_momentum[...] = buffer - feedback * terms[:rows]
    step_scale = step_size * math.sqrt(ROWS / RANK)
    new_weight[...] = (weight[...].astype(jnp.float32) - step_scale * terms[rows:]).astype(jnp.bfloat16)


def updated(y_at, blocks, low, spread, weight, gradient, momentum, steps=3):
    rows, cols = weight.shape
    whole = lambda x: pl.BlockSpec(x.shape, lambda i: (0,) * x.ndim)
    part = pl.BlockSpec((rows, cols // steps), lambda i: (0, i))
    return pl.pallas_call(
        update,
        grid=(steps,),
        in_specs=[pl.BlockSpec(memory_space=pltpu.SMEM)]
        + [whole(x) for x in (*blocks, low, spread)]
        + [part, part, part],
        out_specs=[part, part],
        out_shape=[
            jax.ShapeDtypeStruct((rows, cols), jnp.bfloat16),
            jax.ShapeDtypeStruct((rows, cols), jnp.float32),
        ],
        scratch_shapes=[
            pltpu.VMEM((cols, RANK), jnp.bfloat16),
            pltpu.VMEM((2 * rows, RANK), jnp.bfloat16),
        ],
        name="update",
    )(y_at.astype(jnp.int32).reshape(1), *blocks, low, spread, weight, gradient, momentum)


def step(weight, gradient, momentum, right_factor):
    y_at = lax.axis_index("y")
    buffer_low = (momentum + gradient.astype(jnp.float32)).astype(jnp.bfloat16)
    rows, cols = buffer_low.shape
    wide = cols // NY

    old = lax.ppermute(right_factor, ("z", "y"), to_work())
    old = gather(old, "z", NZ).reshape(wide, RANK)

    tall = lax.all_to_all(
        buffer_low.reshape(rows, NY, wide).transpose(1, 0, 2), "y", 0, 0
    ).reshape(NY * rows, wide)

    part = jnp.dot(tall, old, preferred_element_type=jnp.float32)
    part = jnp.sum(lax.all_to_all(part.reshape(NC, -1, RANK), "c", 0, 0), axis=0)
    chips = NY * NX
    part = lax.all_to_all(halves(part).reshape(chips, -1, 128), ("y", "x"), 0, 0)
    own = jnp.sum(part, axis=0) / math.sqrt(COLS)
    left = unhalves(gather(own, ("y", "x"), chips).reshape(-1, 128))
    left = gather(left, "c", NC).reshape(-1, RANK)

    gram = jnp.dot(left.T, left, precision=lax.Precision.HIGHEST)
    blocks = jnp.concatenate([gram[:HALF, :HALF], gram[:HALF, HALF:], gram[HALF:, HALF:]], axis=0)
    pieces = NY * NC
    mine = lax.dynamic_index_in_dim(
        blocks.reshape(pieces, -1, HALF), y_at * NC + lax.axis_index("c"), 0, keepdims=False
    )

    terms = []
    over = left
    for _ in range(3):
        terms.append(lax.reduce_precision(over, 8, 7))
        over = over - terms[-1]
    terms = jnp.concatenate(terms, axis=1).astype(jnp.bfloat16)
    part = lax.dot_general(tall, terms, (((0,), (0,)), ((), ())), preferred_element_type=jnp.float32)
    part = part[:, :RANK] + part[:, RANK : 2 * RANK] + part[:, 2 * RANK :]
    own = wide // NZ
    part = [part[:, k : k + HALF].reshape(NZ, own, HALF) for k in range(0, RANK, HALF)]
    part.append(jnp.broadcast_to(mine[None], (NZ,) + mine.shape))
    part = jnp.sum(lax.all_to_all(jnp.concatenate(part, axis=1), "z", 0, 0), axis=0)
    blocks = gather(part[2 * own :], ("y", "c"), pieces).reshape(3 * HALF, HALF)

    inverse = lower_inverse(blocks)
    right = dot(jnp.concatenate([part[:own], part[own : 2 * own]], axis=1), inverse, ((1,), (1,)))
    mine_low = lax.dynamic_slice_in_dim(left, y_at * rows, rows, 0)
    mine_low = dot(mine_low, inverse, ((1,), (1,))).astype(jnp.bfloat16)

    sent = gather(right.astype(jnp.bfloat16), "z", NZ).reshape(wide, RANK)
    rights = spread_y(sent)
    squares = sent.astype(jnp.float32)
    squares = jnp.sum(squares * squares, axis=0).reshape(2, 128)
    colsq = jnp.sum(gather(jnp.pad(squares, ((0, 6), (0, 0))), SLAB, NSLAB), axis=0)
    spread = jnp.sqrt(colsq[:2].reshape(1, RANK) / COLS + epsilon)

    new_right = (right / spread).astype(jnp.bfloat16)
    new_right = lax.ppermute(new_right, ("z", "y"), [(b, a) for a, b in to_work()])
    new_weight, new_momentum = updated(y_at, rights, mine_low, spread, weight, gradient, momentum)
    return (new_weight, new_momentum, new_right)


def solution(mesh):
    grid = Mesh(mesh.devices.reshape(NZ, NY, NX, NC), ("z", "y", "x", "c"))
    row, col = ("z", "y"), ("x", "c")
    placed = (P(row, col), P(row, col), P(row, col), P(col + row, None))
    return jax.shard_map(
        step,
        mesh=grid,
        in_specs=placed,
        out_specs=(P(row, col), P(row, col), P(col + row, None)),
        check_vma=False,
    )
```

```python
import math

import jax
import jax.numpy as jnp
from jax import lax
from jax.experimental import pallas as pl
from jax.experimental.pallas import tpu as pltpu
from jax.sharding import Mesh, PartitionSpec as P


ROWS = 9216
COLS = 27648
RANK = 256

shift_frac = 0.001
epsilon = 1e-06
feedback = 0.05
step_size = 0.5

NZ, NY, NX, NC = 12, 8, 4, 2
SLAB = ("y", "x", "c")
NSLAB = NY * NX * NC


HALF = 128
GROUP = 8


def inverse_lower(block):
    tiles = HALF // 8
    at = lax.broadcasted_iota(jnp.int32, (8, HALF), 0)
    lane = lax.broadcasted_iota(jnp.int32, (8, HALF), 1)
    a = [block[8 * t : 8 * t + 8] for t in range(tiles)]
    w = [jnp.where(lane == at + 8 * t, 1.0, 0.0) for t in range(tiles)]
    roots = [jnp.zeros((8, HALF), jnp.float32) for _ in range(tiles)]
    full = lambda v: jnp.broadcast_to(v, (8, HALF))
    for k in range(0, HALF, GROUP):
        own, base = k // 8, k % 8
        r = [full(a[own][base + j : base + j + 1]) for j in range(GROUP)]
        v = [full(w[own][base + j : base + j + 1]) for j in range(GROUP)]
        s = {}
        for i in range(GROUP):
            for j in range(i, GROUP):
                s[i, j] = full(r[i][:, k + j : k + j + 1])
        c = {}
        for t in range(own, tiles):
            for j in range(GROUP):
                c[t, j] = full(a[t][:, k + j : k + j + 1])
        inv = []
        for j in range(GROUP):
            if j % 2:
                inv.append(after)
            else:
                inv.append(1.0 / s[j, j])
                after = s[j, j] / (s[j, j] * s[j + 1, j + 1] - s[j, j + 1] * s[j, j + 1])
            for i in range(j + 1, GROUP):
                f = s[j, i] * inv[j]
                for m in range(i, GROUP):
                    s[i, m] = s[i, m] - f * s[j, m]
                r[i] = r[i] - f * r[j]
                v[i] = v[i] - f * v[j]
            roots[own] = jnp.where(at == base + j, jnp.sqrt(inv[j]), roots[own])
        for t in range(own, tiles):
            l = []
            for j in range(GROUP):
                x = c[t, j]
                for i in range(j):
                    x = x - l[i] * s[i, j]
                x = x * inv[j]
                if t == own:
                    x = jnp.where(at > base + j, x, 0.0)
                l.append(x)
            for j in range(GROUP):
                a[t] = a[t] - l[j] * r[j]
                w[t] = w[t] - l[j] * v[j]
    return jnp.concatenate([w[t] * roots[t] for t in range(tiles)], axis=0)


def dot(x, y, dims):
    return lax.dot_general(x, y, (dims, ((), ())), precision=lax.Precision.HIGHEST, preferred_element_type=jnp.float32)


def kernel(g_ref, out_ref, work_ref, inv_ref):
    first, across, last = (g_ref.at[k * HALF : (k + 1) * HALF] for k in range(3))
    row = lax.broadcasted_iota(jnp.int32, (HALF, HALF), 0)
    eye = row == lax.broadcasted_iota(jnp.int32, (HALF, HALF), 1)
    alpha = (2 * HALF) / jnp.sum(jnp.where(eye, first[...] + last[...], 0.0), keepdims=True)
    shifted = jnp.where(eye, shift_frac, 0.0)
    work_ref[...] = first[...] * alpha + shifted

    def step(b, carry):
        inv_ref[pl.ds(b * HALF, HALF), :] = inverse_lower(work_ref[...])

        @pl.when(b == 0)
        def _():
            z = dot(inv_ref[0:HALF, :], across[...] * alpha, ((1,), (0,)))
            out_ref[HALF:, 0:HALF] = dot(z, inv_ref[0:HALF, :], ((0,), (0,)))
            work_ref[...] = last[...] * alpha + shifted - dot(z, z, ((0,), (0,)))

        return carry

    lax.fori_loop(0, 2, step, 0)
    scale = jnp.sqrt(alpha)
    out_ref[0:HALF, 0:HALF] = inv_ref[0:HALF, :] * scale
    out_ref[0:HALF, HALF:] = jnp.zeros((HALF, HALF), jnp.float32)
    out_ref[HALF:, HALF:] = inv_ref[HALF:, :] * scale
    out_ref[HALF:, 0:HALF] = -scale * dot(inv_ref[HALF:, :], out_ref[HALF:, 0:HALF], ((1,), (0,)))


def lower_inverse(g):
    return pl.pallas_call(
        kernel,
        in_specs=[pl.BlockSpec(memory_space=pltpu.VMEM)],
        out_specs=pl.BlockSpec(memory_space=pltpu.VMEM),
        out_shape=jax.ShapeDtypeStruct((2 * HALF, 2 * HALF), jnp.float32),
        scratch_shapes=[
            pltpu.VMEM((HALF, HALF), jnp.float32),
            pltpu.VMEM((2 * HALF, HALF), jnp.float32),
        ],
        name="lower_inverse",
    )(g)


def gather(x, axes, n):
    return lax.all_to_all(jnp.broadcast_to(x[None], (n,) + x.shape), axes, 0, 0)


def halves(x):
    return jnp.concatenate([x[:, :128], x[:, 128:]], axis=0)


def unhalves(x):
    n = x.shape[0] // 2
    return jnp.concatenate([x[:n], x[n:]], axis=1)


def to_work():
    pairs = []
    for z in range(NZ):
        for y in range(NY):
            k = y * NZ + z
            pairs.append((k, z * NY + y))
    return pairs


def shift(x, by):
    return lax.ppermute(x, "y", [(i, (i + by) % NY) for i in range(NY)])


FROM = ((-3, 0, 3), (-4, -1, 2), (-2, 1))


def spread_y(x):
    above, below = shift(x, 3), shift(x, -3)
    first = jnp.stack([above, x, below])
    return first, shift(first, 1), shift(first[:2], -1)


def update(y_ref, first, second, third, low, spread, own_right, weight, gradient, momentum, new_weight, new_momentum, new_right, right, both):
    wide = first.shape[1]
    rows = low.shape[0]
    for blocks, places in zip((first, second, third), FROM):
        for j, place in enumerate(places):
            block = lax.rem(y_ref[0] + (place + NY), NY)
            right[pl.ds(pl.multiple_of(block * wide, 16), wide), :] = blocks[j]
    both[0:rows, :] = low[...]
    both[rows:, :] = (low[...].astype(jnp.float32) / spread[...]).astype(jnp.bfloat16)
    new_right[...] = own_right[...]
    step_scale = step_size * math.sqrt(ROWS / RANK)
    chunk = weight.shape[1] // 3
    for at in range(0, weight.shape[1], chunk):
        part = slice(at, at + chunk)
        terms = lax.dot_general(
            both[...], right[part, :], (((1,), (1,)), ((), ())), preferred_element_type=jnp.float32
        )
        buffer = momentum[:, part] + gradient[:, part].astype(jnp.float32)
        new_momentum[:, part] = buffer - feedback * terms[:rows]
        new_weight[:, part] = (weight[:, part].astype(jnp.float32) - step_scale * terms[rows:]).astype(jnp.bfloat16)


def updated(y_at, blocks, low, spread, own_right, weight, gradient, momentum):
    rows, cols = weight.shape
    args = (*blocks, low, spread, own_right, weight, gradient, momentum)
    return pl.pallas_call(
        update,
        in_specs=[pl.BlockSpec(memory_space=pltpu.SMEM)] + [pl.BlockSpec(memory_space=pltpu.VMEM)] * len(args),
        out_specs=[pl.BlockSpec(memory_space=pltpu.VMEM)] * 3,
        out_shape=[
            jax.ShapeDtypeStruct((rows, cols), jnp.bfloat16),
            jax.ShapeDtypeStruct((rows, cols), jnp.float32),
            jax.ShapeDtypeStruct(own_right.shape, jnp.bfloat16),
        ],
        scratch_shapes=[
            pltpu.VMEM((cols, RANK), jnp.bfloat16),
            pltpu.VMEM((2 * rows, RANK), jnp.bfloat16),
        ],
        name="update",
    )(y_at.astype(jnp.int32).reshape(1), *args)


def step(weight, gradient, momentum, right_factor):
    y_at = lax.axis_index("y")
    buffer_low = (momentum + gradient.astype(jnp.float32)).astype(jnp.bfloat16)
    rows, cols = buffer_low.shape
    wide = cols // NY

    old = lax.ppermute(right_factor, ("z", "y"), to_work())
    old = gather(old, "z", NZ).reshape(wide, RANK)

    tall = lax.all_to_all(
        buffer_low.reshape(rows, NY, wide).transpose(1, 0, 2), "y", 0, 0
    ).reshape(NY * rows, wide)

    part = jnp.dot(tall, old, preferred_element_type=jnp.float32)
    part = jnp.sum(lax.all_to_all(part.reshape(NC, -1, RANK), "c", 0, 0), axis=0)
    chips = NY * NX
    part = lax.all_to_all(halves(part).reshape(chips, -1, 128), ("y", "x"), 0, 0)
    own = jnp.sum(part, axis=0) / math.sqrt(COLS)
    left = unhalves(gather(own, ("y", "x"), chips).reshape(-1, 128))
    left = gather(left, "c", NC).reshape(-1, RANK)

    gram = jnp.dot(left.T, left, precision=lax.Precision.HIGHEST)
    blocks = jnp.concatenate([gram[:HALF, :HALF], gram[:HALF, HALF:], gram[HALF:, HALF:]], axis=0)
    pieces = NY * NC
    mine = lax.dynamic_index_in_dim(
        blocks.reshape(pieces, -1, HALF), y_at * NC + lax.axis_index("c"), 0, keepdims=False
    )

    terms = []
    over = left
    for _ in range(3):
        terms.append(lax.reduce_precision(over, 8, 7))
        over = over - terms[-1]
    terms = jnp.concatenate(terms, axis=1).astype(jnp.bfloat16)
    part = lax.dot_general(tall, terms, (((0,), (0,)), ((), ())), preferred_element_type=jnp.float32)
    part = part[:, :RANK] + part[:, RANK : 2 * RANK] + part[:, 2 * RANK :]
    own = wide // NZ
    part = [part[:, k : k + HALF].reshape(NZ, own, HALF) for k in range(0, RANK, HALF)]
    part.append(jnp.broadcast_to(mine[None], (NZ,) + mine.shape))
    part = jnp.sum(lax.all_to_all(jnp.concatenate(part, axis=1), "z", 0, 0), axis=0)
    blocks = gather(part[2 * own :], ("y", "c"), pieces).reshape(3 * HALF, HALF)

    inverse = lower_inverse(blocks)
    right = dot(jnp.concatenate([part[:own], part[own : 2 * own]], axis=1), inverse, ((1,), (1,)))
    mine_low = lax.dynamic_slice_in_dim(left, y_at * rows, rows, 0)
    mine_low = dot(mine_low, inverse, ((1,), (1,))).astype(jnp.bfloat16)

    sent = gather(right.astype(jnp.bfloat16), "z", NZ).reshape(wide, RANK)
    rights = spread_y(sent)
    squares = sent.astype(jnp.float32)
    squares = jnp.sum(squares * squares, axis=0).reshape(2, 128)
    squares = gather(squares, SLAB, NSLAB)
    colsq = jnp.sum(squares, axis=0)
    spread = jnp.sqrt(colsq.reshape(1, RANK) / COLS + epsilon)

    new_right = (right / spread).astype(jnp.bfloat16)
    new_right = lax.ppermute(new_right, ("z", "y"), [(b, a) for a, b in to_work()])
    return tuple(updated(y_at, rights, mine_low, spread, new_right, weight, gradient, momentum))


def solution(mesh):
    grid = Mesh(mesh.devices.reshape(NZ, NY, NX, NC), ("z", "y", "x", "c"))
    row, col = ("z", "y"), ("x", "c")
    placed = (P(row, col), P(row, col), P(row, col), P(col + row, None))
    return jax.shard_map(
        step,
        mesh=grid,
        in_specs=placed,
        out_specs=(P(row, col), P(row, col), P(col + row, None)),
        check_vma=False,
    )
```

```python
import math

import jax
import jax.numpy as jnp
from jax import lax
from jax.experimental import pallas as pl
from jax.experimental.pallas import tpu as pltpu
from jax.sharding import Mesh, PartitionSpec as P


ROWS = 9216
COLS = 27648
RANK = 256

shift_frac = 0.001
epsilon = 1e-06
feedback = 0.05
step_size = 0.5

NZ, NY, NX, NC = 12, 8, 4, 2


HALF = 128
GROUP = 8


def inverse_lower(block):
    tiles = HALF // 8
    at = lax.broadcasted_iota(jnp.int32, (8, HALF), 0)
    lane = lax.broadcasted_iota(jnp.int32, (8, HALF), 1)
    a = [block[8 * t : 8 * t + 8] for t in range(tiles)]
    w = [jnp.where(lane == at + 8 * t, 1.0, 0.0) for t in range(tiles)]
    roots = [jnp.zeros((8, HALF), jnp.float32) for _ in range(tiles)]
    full = lambda v: jnp.broadcast_to(v, (8, HALF))
    for k in range(0, HALF, GROUP):
        own, base = k // 8, k % 8
        r = [full(a[own][base + j : base + j + 1]) for j in range(GROUP)]
        v = [full(w[own][base + j : base + j + 1]) for j in range(GROUP)]
        s = {}
        for i in range(GROUP):
            for j in range(i, GROUP):
                s[i, j] = full(r[i][:, k + j : k + j + 1])
        c = {}
        for t in range(own, tiles):
            for j in range(GROUP):
                c[t, j] = full(a[t][:, k + j : k + j + 1])
        inv = []
        for j in range(GROUP):
            if j % 2:
                inv.append(after)
            else:
                inv.append(1.0 / s[j, j])
                after = s[j, j] / (s[j, j] * s[j + 1, j + 1] - s[j, j + 1] * s[j, j + 1])
            for i in range(j + 1, GROUP):
                f = s[j, i] * inv[j]
                for m in range(i, GROUP):
                    s[i, m] = s[i, m] - f * s[j, m]
                r[i] = r[i] - f * r[j]
                v[i] = v[i] - f * v[j]
            roots[own] = jnp.where(at == base + j, jnp.sqrt(inv[j]), roots[own])
        for t in range(own, tiles):
            l = []
            for j in range(GROUP):
                x = c[t, j]
                for i in range(j):
                    x = x - l[i] * s[i, j]
                x = x * inv[j]
                if t == own:
                    x = jnp.where(at > base + j, x, 0.0)
                l.append(x)
            for j in range(GROUP):
                a[t] = a[t] - l[j] * r[j]
                w[t] = w[t] - l[j] * v[j]
    return jnp.concatenate([w[t] * roots[t] for t in range(tiles)], axis=0)


def dot(x, y, dims):
    return lax.dot_general(x, y, (dims, ((), ())), precision=lax.Precision.HIGHEST, preferred_element_type=jnp.float32)


def kernel(g_ref, low_ref, high_ref, out_ref, right_ref, work_ref, inv_ref):
    first, across, last = (g_ref.at[k * HALF : (k + 1) * HALF] for k in range(3))
    row = lax.broadcasted_iota(jnp.int32, (HALF, HALF), 0)
    eye = row == lax.broadcasted_iota(jnp.int32, (HALF, HALF), 1)
    alpha = (2 * HALF) / jnp.sum(jnp.where(eye, first[...] + last[...], 0.0), keepdims=True)
    shifted = jnp.where(eye, shift_frac, 0.0)
    work_ref[...] = first[...] * alpha + shifted

    def step(b, carry):
        inv_ref[pl.ds(b * HALF, HALF), :] = inverse_lower(work_ref[...])

        @pl.when(b == 0)
        def _():
            z = dot(inv_ref[0:HALF, :], across[...] * alpha, ((1,), (0,)))
            out_ref[HALF:, 0:HALF] = dot(z, inv_ref[0:HALF, :], ((0,), (0,)))
            work_ref[...] = last[...] * alpha + shifted - dot(z, z, ((0,), (0,)))

        return carry

    lax.fori_loop(0, 2, step, 0)
    scale = jnp.sqrt(alpha)
    out_ref[0:HALF, 0:HALF] = inv_ref[0:HALF, :] * scale
    out_ref[0:HALF, HALF:] = jnp.zeros((HALF, HALF), jnp.float32)
    out_ref[HALF:, HALF:] = inv_ref[HALF:, :] * scale
    out_ref[HALF:, 0:HALF] = -scale * dot(inv_ref[HALF:, :], out_ref[HALF:, 0:HALF], ((1,), (0,)))
    right_ref[:, 0:HALF] = dot(low_ref[...], out_ref[0:HALF, 0:HALF], ((1,), (1,)))
    right_ref[:, HALF:] = dot(low_ref[...], out_ref[HALF:, 0:HALF], ((1,), (1,))) + dot(high_ref[...], out_ref[HALF:, HALF:], ((1,), (1,)))


def lower_inverse(g, low, high):
    return pl.pallas_call(
        kernel,
        out_shape=[
            jax.ShapeDtypeStruct((2 * HALF, 2 * HALF), jnp.float32),
            jax.ShapeDtypeStruct((low.shape[0], 2 * HALF), jnp.float32),
        ],
        scratch_shapes=[
            pltpu.VMEM((HALF, HALF), jnp.float32),
            pltpu.VMEM((2 * HALF, HALF), jnp.float32),
        ],
        name="lower_inverse",
    )(g, low, high)


def gather(x, axes, n):
    return lax.all_to_all(jnp.broadcast_to(x[None], (n,) + x.shape), axes, 0, 0)


def halves(x):
    return jnp.concatenate([x[:, :128], x[:, 128:]], axis=0)


def unhalves(x):
    n = x.shape[0] // 2
    return jnp.concatenate([x[:n], x[n:]], axis=1)


def to_work():
    pairs = []
    for z in range(NZ):
        for y in range(NY):
            k = y * NZ + z
            pairs.append((k, z * NY + y))
    return pairs


def shift(x, by):
    return lax.ppermute(x, "y", [(i, (i + by) % NY) for i in range(NY)])


FROM = ((-3, 0, 3), (-4, -1, 2), (-2, 1))


def spread_y(x):
    above, below = shift(x, 3), shift(x, -3)
    first = jnp.stack([above, x, below])
    return first, shift(first, 1), shift(first[:2], -1)


def update(y_ref, first, second, third, low, spread, own_right, weight, gradient, momentum, new_weight, new_momentum, new_right, right, both):
    wide = first.shape[1]
    rows = low.shape[0]
    for blocks, places in zip((first, second, third), FROM):
        for j, place in enumerate(places):
            block = lax.rem(y_ref[0] + (place + NY), NY)
            right[pl.ds(pl.multiple_of(block * wide, 16), wide), :] = blocks[j]
    both[0:rows, :] = low[...]
    both[rows:, :] = (low[...].astype(jnp.float32) / spread[...]).astype(jnp.bfloat16)
    new_right[...] = own_right[...]
    step_scale = step_size * math.sqrt(ROWS / RANK)
    chunk = weight.shape[1] // 3
    for at in range(0, weight.shape[1], chunk):
        part = slice(at, at + chunk)
        terms = lax.dot_general(
            both[...], right[part, :], (((1,), (1,)), ((), ())), preferred_element_type=jnp.float32
        )
        buffer = momentum[:, part] + gradient[:, part].astype(jnp.float32)
        new_momentum[:, part] = buffer - feedback * terms[:rows]
        new_weight[:, part] = (weight[:, part].astype(jnp.float32) - step_scale * terms[rows:]).astype(jnp.bfloat16)


def updated(y_at, blocks, low, spread, own_right, weight, gradient, momentum):
    rows, cols = weight.shape
    args = [pltpu.with_memory_space_constraint(x, pltpu.VMEM) for x in (weight, gradient, momentum)]
    args = (*blocks, low, spread, own_right, *args)
    return pl.pallas_call(
        update,
        in_specs=[pl.BlockSpec(memory_space=pltpu.SMEM)] + [pl.BlockSpec(memory_space=pltpu.VMEM)] * len(args),
        out_specs=[pl.BlockSpec(memory_space=pltpu.VMEM)] * 3,
        out_shape=[
            jax.ShapeDtypeStruct((rows, cols), jnp.bfloat16),
            jax.ShapeDtypeStruct((rows, cols), jnp.float32),
            jax.ShapeDtypeStruct(own_right.shape, jnp.bfloat16),
        ],
        scratch_shapes=[
            pltpu.VMEM((cols, RANK), jnp.bfloat16),
            pltpu.VMEM((2 * rows, RANK), jnp.bfloat16),
        ],
        compiler_params=pltpu.CompilerParams(vmem_limit_bytes=20 << 20),
        name="update",
    )(y_at.astype(jnp.int32).reshape(1), *args)


def step(weight, gradient, momentum, right_factor):
    y_at = lax.axis_index("y")
    buffer_low = (momentum + gradient.astype(jnp.float32)).astype(jnp.bfloat16)
    rows, cols = buffer_low.shape
    wide = cols // NY

    old = lax.ppermute(right_factor, ("z", "y"), to_work())
    old = gather(old, "z", NZ).reshape(wide, RANK)

    tall = lax.all_to_all(
        buffer_low.reshape(rows, NY, wide).transpose(1, 0, 2), "y", 0, 0
    ).reshape(NY * rows, wide)

    part = jnp.dot(tall, old, preferred_element_type=jnp.float32)
    part = jnp.sum(lax.all_to_all(part.reshape(NC, -1, RANK), "c", 0, 0), axis=0)
    chips = NY * NX
    part = lax.all_to_all(halves(part).reshape(chips, -1, 128), ("y", "x"), 0, 0)
    own = jnp.sum(part, axis=0) / math.sqrt(COLS)
    left = unhalves(gather(own, ("y", "x"), chips).reshape(-1, 128))
    left = gather(left, "c", NC).reshape(-1, RANK)

    gram = jnp.dot(left.T, left, precision=lax.Precision.HIGHEST)
    blocks = jnp.concatenate([gram[:HALF, :HALF], gram[:HALF, HALF:], gram[HALF:, HALF:]], axis=0)
    pieces = NY * NC
    mine = lax.dynamic_index_in_dim(
        blocks.reshape(pieces, -1, HALF), y_at * NC + lax.axis_index("c"), 0, keepdims=False
    )

    terms = []
    over = left
    for _ in range(3):
        terms.append(lax.reduce_precision(over, 8, 7))
        over = over - terms[-1]
    terms = jnp.concatenate(terms, axis=1).astype(jnp.bfloat16)
    part = lax.dot_general(tall, terms, (((0,), (0,)), ((), ())), preferred_element_type=jnp.float32)
    part = part[:, :RANK] + part[:, RANK : 2 * RANK] + part[:, 2 * RANK :]
    own = wide // NZ
    part = [part[:, k : k + HALF].reshape(NZ, own, HALF) for k in range(0, RANK, HALF)]
    part.append(jnp.broadcast_to(mine[None], (NZ,) + mine.shape))
    part = jnp.sum(lax.all_to_all(jnp.concatenate(part, axis=1), "z", 0, 0), axis=0)
    blocks = gather(part[2 * own :], ("y", "c"), pieces).reshape(3 * HALF, HALF)

    inverse, right = lower_inverse(blocks, part[:own], part[own : 2 * own])
    mine_low = lax.dynamic_slice_in_dim(left, y_at * rows, rows, 0)
    mine_low = dot(mine_low, inverse, ((1,), (1,))).astype(jnp.bfloat16)

    sent = gather(right.astype(jnp.bfloat16), "z", NZ).reshape(wide, RANK)
    rights = spread_y(sent)
    squares = sent.astype(jnp.float32)
    squares = jnp.sum(squares * squares, axis=0).reshape(2, 128)
    squares = gather(squares, ("x", "c"), NX * NC)
    squares = jnp.sum(squares, axis=0)
    colsq = jnp.sum(gather(squares, "y", NY), axis=0)
    spread = jnp.sqrt(colsq.reshape(1, RANK) / COLS + epsilon)

    new_right = (right / spread).astype(jnp.bfloat16)
    new_right = lax.ppermute(new_right, ("z", "y"), [(b, a) for a, b in to_work()])
    return tuple(updated(y_at, rights, mine_low, spread, new_right, weight, gradient, momentum))


def solution(mesh):
    grid = Mesh(mesh.devices.reshape(NZ, NY, NX, NC), ("z", "y", "x", "c"))
    row, col = ("z", "y"), ("x", "c")
    placed = (P(row, col), P(row, col), P(row, col), P(col + row, None))
    return jax.shard_map(
        step,
        mesh=grid,
        in_specs=placed,
        out_specs=(P(row, col), P(row, col), P(col + row, None)),
        check_vma=False,
    )
```

```python
import math

import jax
import jax.numpy as jnp
from jax import lax
from jax.experimental import pallas as pl
from jax.experimental.pallas import tpu as pltpu
from jax.sharding import Mesh, PartitionSpec as P


ROWS = 9216
COLS = 27648
RANK = 256

shift_frac = 0.001
epsilon = 1e-06
feedback = 0.05
step_size = 0.5

NZ, NY, NX, NC = 12, 8, 4, 2
SLAB = ("y", "x", "c")
NSLAB = NY * NX * NC


HALF = 128
GROUP = 8


def inverse_lower(block):
    tiles = HALF // 8
    at = lax.broadcasted_iota(jnp.int32, (8, HALF), 0)
    lane = lax.broadcasted_iota(jnp.int32, (8, HALF), 1)
    a = [block[8 * t : 8 * t + 8] for t in range(tiles)]
    w = [jnp.where(lane == at + 8 * t, 1.0, 0.0) for t in range(tiles)]
    roots = [jnp.zeros((8, HALF), jnp.float32) for _ in range(tiles)]
    full = lambda v: jnp.broadcast_to(v, (8, HALF))
    for k in range(0, HALF, GROUP):
        own, base = k // 8, k % 8
        r = [full(a[own][base + j : base + j + 1]) for j in range(GROUP)]
        v = [full(w[own][base + j : base + j + 1]) for j in range(GROUP)]
        s = {}
        for i in range(GROUP):
            for j in range(i, GROUP):
                s[i, j] = full(r[i][:, k + j : k + j + 1])
        c = {}
        for t in range(own, tiles):
            for j in range(GROUP):
                c[t, j] = full(a[t][:, k + j : k + j + 1])
        inv = []
        for j in range(GROUP):
            if j % 2:
                inv.append(after)
            else:
                inv.append(1.0 / s[j, j])
                after = s[j, j] / (s[j, j] * s[j + 1, j + 1] - s[j, j + 1] * s[j, j + 1])
            for i in range(j + 1, GROUP):
                f = s[j, i] * inv[j]
                for m in range(i, GROUP):
                    s[i, m] = s[i, m] - f * s[j, m]
                r[i] = r[i] - f * r[j]
                v[i] = v[i] - f * v[j]
            roots[own] = jnp.where(at == base + j, jnp.sqrt(inv[j]), roots[own])
        for t in range(own, tiles):
            l = []
            for j in range(GROUP):
                x = c[t, j]
                for i in range(j):
                    x = x - l[i] * s[i, j]
                x = x * inv[j]
                if t == own:
                    x = jnp.where(at > base + j, x, 0.0)
                l.append(x)
            for j in range(GROUP):
                a[t] = a[t] - l[j] * r[j]
                w[t] = w[t] - l[j] * v[j]
    return jnp.concatenate([w[t] * roots[t] for t in range(tiles)], axis=0)


def dot(x, y, dims):
    return lax.dot_general(x, y, (dims, ((), ())), precision=lax.Precision.HIGHEST, preferred_element_type=jnp.float32)


def kernel(g_ref, low_ref, high_ref, out_ref, right_ref, work_ref, inv_ref):
    first, across, last = (g_ref.at[k * HALF : (k + 1) * HALF] for k in range(3))
    row = lax.broadcasted_iota(jnp.int32, (HALF, HALF), 0)
    eye = row == lax.broadcasted_iota(jnp.int32, (HALF, HALF), 1)
    alpha = (2 * HALF) / jnp.sum(jnp.where(eye, first[...] + last[...], 0.0), keepdims=True)
    shifted = jnp.where(eye, shift_frac, 0.0)
    work_ref[...] = first[...] * alpha + shifted

    def step(b, carry):
        inv_ref[pl.ds(b * HALF, HALF), :] = inverse_lower(work_ref[...])

        @pl.when(b == 0)
        def _():
            z = dot(inv_ref[0:HALF, :], across[...] * alpha, ((1,), (0,)))
            out_ref[HALF:, 0:HALF] = dot(z, inv_ref[0:HALF, :], ((0,), (0,)))
            work_ref[...] = last[...] * alpha + shifted - dot(z, z, ((0,), (0,)))

        return carry

    lax.fori_loop(0, 2, step, 0)
    scale = jnp.sqrt(alpha)
    out_ref[0:HALF, 0:HALF] = inv_ref[0:HALF, :] * scale
    out_ref[0:HALF, HALF:] = jnp.zeros((HALF, HALF), jnp.float32)
    out_ref[HALF:, HALF:] = inv_ref[HALF:, :] * scale
    out_ref[HALF:, 0:HALF] = -scale * dot(inv_ref[HALF:, :], out_ref[HALF:, 0:HALF], ((1,), (0,)))
    right_ref[:, 0:HALF] = dot(low_ref[...], out_ref[0:HALF, 0:HALF], ((1,), (1,)))
    right_ref[:, HALF:] = dot(low_ref[...], out_ref[HALF:, 0:HALF], ((1,), (1,))) + dot(high_ref[...], out_ref[HALF:, HALF:], ((1,), (1,)))


def lower_inverse(g, low, high):
    return pl.pallas_call(
        kernel,
        in_specs=[pl.BlockSpec(memory_space=pltpu.VMEM)] * 3,
        out_specs=[pl.BlockSpec(memory_space=pltpu.VMEM)] * 2,
        out_shape=[
            jax.ShapeDtypeStruct((2 * HALF, 2 * HALF), jnp.float32),
            jax.ShapeDtypeStruct((low.shape[0], 2 * HALF), jnp.float32),
        ],
        scratch_shapes=[
            pltpu.VMEM((HALF, HALF), jnp.float32),
            pltpu.VMEM((2 * HALF, HALF), jnp.float32),
        ],
        compiler_params=pltpu.CompilerParams(vmem_limit_bytes=8 << 20),
        name="lower_inverse",
    )(g, low, high)


def gather(x, axes, n):
    return lax.all_to_all(jnp.broadcast_to(x[None], (n,) + x.shape), axes, 0, 0)


def halves(x):
    return jnp.concatenate([x[:, :128], x[:, 128:]], axis=0)


def unhalves(x):
    n = x.shape[0] // 2
    return jnp.concatenate([x[:n], x[n:]], axis=1)


def to_work():
    pairs = []
    for z in range(NZ):
        for y in range(NY):
            k = y * NZ + z
            pairs.append((k, z * NY + y))
    return pairs


def shift(x, by):
    return lax.ppermute(x, "y", [(i, (i + by) % NY) for i in range(NY)])


FROM = ((-3, 0, 3), (-4, -1, 2), (-2, 1))


def spread_y(x):
    above, below = shift(x, 3), shift(x, -3)
    first = jnp.stack([above, x, below])
    return first, shift(first, 1), shift(first[:2], -1)


def update(y_ref, first, second, third, low, spread, own_right, weight, gradient, momentum, new_weight, new_momentum, new_right, right, both):
    wide = first.shape[1]
    rows = low.shape[0]
    for blocks, places in zip((first, second, third), FROM):
        for j, place in enumerate(places):
            block = lax.rem(y_ref[0] + (place + NY), NY)
            right[pl.ds(pl.multiple_of(block * wide, 16), wide), :] = blocks[j]
    both[0:rows, :] = low[...]
    both[rows:, :] = (low[...].astype(jnp.float32) / spread[...]).astype(jnp.bfloat16)
    new_right[...] = own_right[...]
    step_scale = step_size * math.sqrt(ROWS / RANK)
    chunk = weight.shape[1] // 3
    for at in range(0, weight.shape[1], chunk):
        part = slice(at, at + chunk)
        terms = lax.dot_general(
            both[...], right[part, :], (((1,), (1,)), ((), ())), preferred_element_type=jnp.float32
        )
        buffer = momentum[:, part] + gradient[:, part].astype(jnp.float32)
        new_momentum[:, part] = buffer - feedback * terms[:rows]
        new_weight[:, part] = (weight[:, part].astype(jnp.float32) - step_scale * terms[rows:]).astype(jnp.bfloat16)


def updated(y_at, blocks, low, spread, own_right, weight, gradient, momentum):
    rows, cols = weight.shape
    args = (*blocks, low, spread, own_right, weight, gradient, momentum)
    return pl.pallas_call(
        update,
        in_specs=[pl.BlockSpec(memory_space=pltpu.SMEM)] + [pl.BlockSpec(memory_space=pltpu.VMEM)] * len(args),
        out_specs=[pl.BlockSpec(memory_space=pltpu.VMEM)] * 3,
        out_shape=[
            jax.ShapeDtypeStruct((rows, cols), jnp.bfloat16),
            jax.ShapeDtypeStruct((rows, cols), jnp.float32),
            jax.ShapeDtypeStruct(own_right.shape, jnp.bfloat16),
        ],
        scratch_shapes=[
            pltpu.VMEM((cols, RANK), jnp.bfloat16),
            pltpu.VMEM((2 * rows, RANK), jnp.bfloat16),
        ],
        name="update",
    )(y_at.astype(jnp.int32).reshape(1), *args)


def step(weight, gradient, momentum, right_factor):
    y_at = lax.axis_index("y")
    buffer_low = (momentum + gradient.astype(jnp.float32)).astype(jnp.bfloat16)
    rows, cols = buffer_low.shape
    wide = cols // NY

    old = lax.ppermute(right_factor, ("z", "y"), to_work())
    old = gather(old, "z", NZ).reshape(wide, RANK)

    tall = lax.all_to_all(
        buffer_low.reshape(rows, NY, wide).transpose(1, 0, 2), "y", 0, 0
    ).reshape(NY * rows, wide)

    part = jnp.dot(tall, old, preferred_element_type=jnp.float32)
    part = jnp.sum(lax.all_to_all(part.reshape(NC, -1, RANK), "c", 0, 0), axis=0)
    chips = NY * NX
    part = lax.all_to_all(halves(part).reshape(chips, -1, 128), ("y", "x"), 0, 0)
    own = jnp.sum(part, axis=0) / math.sqrt(COLS)
    left = unhalves(gather(own, ("y", "x"), chips).reshape(-1, 128))
    left = gather(left, "c", NC).reshape(-1, RANK)

    gram = jnp.dot(left.T, left, precision=lax.Precision.HIGHEST)
    blocks = jnp.concatenate([gram[:HALF, :HALF], gram[:HALF, HALF:], gram[HALF:, HALF:]], axis=0)
    pieces = NY * NC
    mine = lax.dynamic_index_in_dim(
        blocks.reshape(pieces, -1, HALF), y_at * NC + lax.axis_index("c"), 0, keepdims=False
    )

    terms = []
    over = left
    for _ in range(3):
        terms.append(lax.reduce_precision(over, 8, 7))
        over = over - terms[-1]
    terms = jnp.concatenate(terms, axis=1).astype(jnp.bfloat16)
    part = lax.dot_general(tall, terms, (((0,), (0,)), ((), ())), preferred_element_type=jnp.float32)
    part = part[:, :RANK] + part[:, RANK : 2 * RANK] + part[:, 2 * RANK :]
    own = wide // NZ
    part = [part[:, k : k + HALF].reshape(NZ, own, HALF) for k in range(0, RANK, HALF)]
    part.append(jnp.broadcast_to(mine[None], (NZ,) + mine.shape))
    part = jnp.sum(lax.all_to_all(jnp.concatenate(part, axis=1), "z", 0, 0), axis=0)
    blocks = gather(part[2 * own :], ("y", "c"), pieces).reshape(3 * HALF, HALF)

    inverse, right = lower_inverse(blocks, part[:own], part[own : 2 * own])
    mine_low = lax.dynamic_slice_in_dim(left, y_at * rows, rows, 0)
    mine_low = dot(mine_low, inverse, ((1,), (1,))).astype(jnp.bfloat16)

    sent = gather(right.astype(jnp.bfloat16), "z", NZ).reshape(wide, RANK)
    rights = spread_y(sent)
    squares = sent.astype(jnp.float32)
    squares = jnp.sum(squares * squares, axis=0).reshape(2, 128)
    squares = gather(squares, SLAB, NSLAB)
    colsq = jnp.sum(squares, axis=0)
    spread = jnp.sqrt(colsq.reshape(1, RANK) / COLS + epsilon)

    new_right = (right / spread).astype(jnp.bfloat16)
    new_right = lax.ppermute(new_right, ("z", "y"), [(b, a) for a, b in to_work()])
    return tuple(updated(y_at, rights, mine_low, spread, new_right, weight, gradient, momentum))


def solution(mesh):
    grid = Mesh(mesh.devices.reshape(NZ, NY, NX, NC), ("z", "y", "x", "c"))
    row, col = ("z", "y"), ("x", "c")
    placed = (P(row, col), P(row, col), P(row, col), P(col + row, None))
    return jax.shard_map(
        step,
        mesh=grid,
        in_specs=placed,
        out_specs=(P(row, col), P(row, col), P(col + row, None)),
        check_vma=False,
    )
```
